128 devices in a mesh: aux: 16 (over z, x_lo, core), rows: 8 (over y, x_hi).
Axes of the slice: x: 4 (x_hi: 2, x_lo: 2; x = x_hi * 2 + x_lo), y: 4, z: 4, core: 2. Of those that a mesh axis runs over, the one named last changes fastest.
Arguments:
- three_center: bfloat16 [128, 40, 16, 128, 128], P('aux', 'rows'), may hold values from -6 to 6
- coeffs: bfloat16 [16384, 128], P('aux'), may hold values from -0.01171875 to 0.01171875
- sig_blocks: int32 [40, 16], P('rows'), may hold values from 0 to 7
- k_columns: int32 [40, 12], P('rows'), may hold values from 0 to 39, as said below
- owners: int32 [480, 1], P('rows'), may hold values from 0 to 7; in each aligned block of 60 rows (0 to 59, 60 to 119, ...) at most 15 rows name the same one
Outputs:
- exchange_blocks: float32 [960, 128, 128], P('rows', 'aux')
The draws below stay inside these ranges and needn't reach their ends.
Inputs may be any that keep to these rules, and one draw needn't show every extreme that they name: `owners`: among the 60 entries of one rows index, no owner is named more than 15 times. `k_columns`: the 12 entries of one row block are distinct, and the first entry of row block m is m itself.
All inputs are finite; a program needn't handle non-finite values.
Results may differ from the reference program's by a relative error of at most 0.0014.
Values may be sent and summed in bfloat16 or wider, within the bound.
A program may use at most 128 MiB of HBM per device.

```python
import math
import jax
import jax.numpy as jnp
import numpy as np
from jax import lax

BS = 128
OCC = 128
NAUXF = 128
BLK_DEV = 8
RB_DEV = 5
KS = 12
NBLK = 128
ROWBLK = 40
CAP = 15
N_AUX = 16
N_ROWS = 8


def draw_k_columns(key, part):
    keys = jax.random.split(jax.random.fold_in(key, 7), ROWBLK)
    row_ids = jnp.arange(ROWBLK, dtype=jnp.int32)

    def one_row(row_key, row_id):
        others = jax.random.permutation(row_key, ROWBLK - 1).astype(jnp.int32)[:KS - 1]
        others = others + (others >= row_id).astype(jnp.int32)
        return jnp.concatenate([row_id[None], others])
    return jax.vmap(one_row)(keys, row_ids)


def with_ends(array, rng, low, high):
    shape = array.shape
    index_at = [jax.random.randint(jax.random.fold_in(rng, axis), (), 0, shape[axis]) for axis in range(len(shape))]
    array = array.at[tuple(index_at)].set(low)
    longest = shape.index(max(shape))
    index_at[longest] = (index_at[longest] + 1) % shape[longest]
    return array.at[tuple(index_at)].set(high)


def level_of(stream_key, extent, cuts, least, high):
    def one(position, parts):
        draws = jax.random.uniform(jax.random.fold_in(jax.random.fold_in(stream_key, 6), position), (parts,), jnp.float32, least / len(cuts), high / len(cuts))
        return jnp.repeat(jnp.exp(draws), extent[position] // parts).reshape((-1,) + (1,) * (len(extent) - position - 1))

    loudness = one(*cuts[0])
    for cut in cuts[1:]:
        loudness = loudness * one(*cut)
    return loudness


def routed_block(own_key, own, number, rows, number_of, top, most, skew):
    order = jax.random.permutation(own_key, number_of)
    packed, usual = portions_of(number_of, rows * top, most, skew, True), portions_of(number_of, rows * top, most, skew, False)
    places = jnp.arange(number_of)

    def named(tallies, rotation):
        used = int((tallies > 0).sum())
        fixed = max(1, used // 4)
        moved = fixed + (places - fixed + rotation * (used - fixed)) % max(1, number_of - fixed)
        return jnp.zeros((number_of,), jnp.int32).at[order[jnp.where(places < fixed, places, moved)]].set(jnp.asarray(tallies, jnp.int32))

    tallies = jnp.where(number % 4 == 0, named(packed, number // 4), named(usual, number - number // 4 - 1))
    mixed = jax.random.permutation(jax.random.fold_in(own, 3), number_of)
    giver, taker = mixed[0:number_of // 2 * 2:2], mixed[1:number_of // 2 * 2:2]
    slack = jnp.minimum(tallies[giver] - 1, most - tallies[taker]) // 2
    slack = jnp.where((giver == order[0]) | (taker == order[0]) | (tallies[taker] == 0), 0, jnp.maximum(slack, 0))
    moved = jax.random.randint(jax.random.fold_in(own, 4), (number_of // 2,), 0, 1 << 20) % (slack + 1)
    tallies = tallies.at[giver].add(-moved).at[taker].add(moved)
    items = jnp.searchsorted(jnp.cumsum(tallies), jnp.arange(rows * top), side="right").astype(jnp.int32)
    grid = items.reshape(top, rows).T
    grid = grid[jax.random.permutation(jax.random.fold_in(own, 1), rows)]
    rotation = jax.random.randint(jax.random.fold_in(own, 2), (rows, 1), 0, top)
    return jnp.take_along_axis(grid, (jnp.arange(top)[None, :] + rotation) % top, axis=1)


def portions_of(amount, total, limit, lean, full):
    weights = [(1 << 20) // math.isqrt(rank ** lean) + 1 for rank in range(1, amount + 1)]
    largest = limit if full else min(limit, max(-(-total // amount), total * weights[0] // sum(weights)))
    least = 1 if total - largest >= amount - 1 else 0
    given, spare = [largest] + [least] * (amount - 1), total - largest - least * (amount - 1)
    while spare > 0:
        free = [i for i in range(1, amount) if given[i] < largest] or [i for i in range(1, amount) if given[i] < limit]
        pool, left = sum([weights[i] for i in free]), spare
        for i in free:
            more = min(limit - given[i], max(1, left * weights[i] // pool), spare)
            given[i] = given[i] + more
            spare = spare - more
    return np.array(given)


def scatter_about(key, shape, deviation, bound, shards=(), held_as=jnp.bfloat16):
    values = deviation * jax.random.normal(key, shape, jnp.float32)
    if shards:
        values = values * level_of(key, shape, shards, -0.22, 0.18)
    return jnp.clip(values, -bound, bound).astype(held_as)


def setup_inputs(seed: int = 0) -> dict:
    seeds = jax.random.split(jax.random.key(seed), 6)
    three_center = scatter_about(seeds[0], (NAUXF, ROWBLK, N_AUX, BS, BS), 1.0, 6.0, ((0, 16), (1, 8)))
    coeffs = scatter_about(seeds[1], (NBLK * BS, OCC), (BS * N_AUX * NAUXF) ** -0.5, 0.01171875, ((0, 16),))
    sig_blocks = with_ends(jax.random.randint(seeds[2], (ROWBLK, N_AUX), 0, BLK_DEV), jax.random.fold_in(seeds[2], 1), 0, BLK_DEV - 1).astype(jnp.int32)
    k_columns = draw_k_columns(jax.random.fold_in(seeds[5], 71), 0)
    owners_keys = jax.random.split(jax.random.fold_in(seeds[4], 1), (ROWBLK * KS) // (RB_DEV * KS))
    owners_turns = jax.random.permutation(jax.random.fold_in(seeds[4], 3), (ROWBLK * KS) // (RB_DEV * KS))
    owners = jax.vmap(lambda own, number: routed_block(jax.random.fold_in(seeds[4], 2), own, number, RB_DEV * KS, N_ROWS, 1, CAP, 2))(owners_keys, owners_turns).reshape((ROWBLK * KS, 1))
    return dict(three_center=three_center, coeffs=coeffs, sig_blocks=sig_blocks, k_columns=k_columns, owners=owners)


def reference(three_center, coeffs, sig_blocks, k_columns, owners):
    blocks = coeffs.reshape(NBLK, BS, OCC)
    wanted = sig_blocks + (jnp.arange(N_AUX, dtype=jnp.int32) * BLK_DEV)[None, :]

    def one_row(index):
        slab = three_center[:, index].astype(jnp.float32)
        picked = blocks[wanted[index]].astype(jnp.float32)
        return jnp.einsum("pqab,qbo->pao", slab, picked).astype(jnp.bfloat16)

    half = lax.map(one_row, jnp.arange(ROWBLK, dtype=jnp.int32))
    flat_cols = k_columns.reshape(ROWBLK * KS)

    def one_block(flat):
        left = half[flat // KS].astype(jnp.float32)
        right = half[flat_cols[flat]].astype(jnp.float32)
        return jnp.einsum("pai,pbi->ab", left, right)

    partial_value = lax.map(one_block, jnp.arange(ROWBLK * KS, dtype=jnp.int32))
    owner_ids = owners[:, 0].reshape(N_ROWS, RB_DEV * KS)
    onehot = (owner_ids[:, :, None] == jnp.arange(N_ROWS, dtype=jnp.int32)[None, None, :]).astype(jnp.int32)
    ranks = jnp.sum(jnp.cumsum(onehot, axis=1) * onehot, axis=2) - 1
    sources = jnp.broadcast_to(jnp.arange(N_ROWS, dtype=jnp.int32)[:, None], owner_ids.shape)
    target = ((owner_ids * N_ROWS + sources) * CAP + ranks).reshape(ROWBLK * KS)
    result = jnp.zeros((N_ROWS * N_ROWS * CAP, BS, BS), jnp.float32)
    return result.at[target].set(partial_value)
```

```python
import jax
import jax.numpy as jnp
from jax import lax
from jax.experimental import pallas as pl
from jax.experimental.pallas import tpu as pltpu
from jax.sharding import PartitionSpec as P

BS = 128
OCC = 128
BLK_DEV = 8
RB = 5
KS = 12
CAP = 15
F32 = jnp.float32
BF16 = jnp.bfloat16


def remote(src, dst, send_sem, recv_sem, device):
    return pltpu.make_async_remote_copy(
        src_ref=src,
        dst_ref=dst,
        send_sem=send_sem,
        recv_sem=recv_sem,
        device_id=device,
        device_id_type=pl.DeviceIdType.MESH,
    )


def kernel(
    t_hbm,
    coeff_ref,
    sig_ref,
    cols_ref,
    slot_ref,
    out_ref,
    t_v,
    picks,
    h_all,
    cols_mine,
    cols_got,
    cols_sm,
    part,
    core_in,
    r1a,
    r1b,
    r2a,
    r2b,
    red,
    abuf,
    t_sem,
    p_send,
    p_recv,
    b_send,
    b_recv,
    x_send,
    x_recv,
    k_sem,
    y_send,
    y_recv,
    c_send,
    c_recv,
    r_send,
    r_recv,
    a_send,
    a_recv,
):
    aux = lax.axis_index("aux")
    rows = lax.axis_index("rows")
    z, xl, c = aux // 4, (aux // 2) % 2, aux % 2
    y, xh = rows // 2, rows % 2
    x = xh * 2 + xl
    zx = aux // 2

    def chip(px, py, pz, core):
        return {"aux": pz * 4 + (px % 2) * 2 + core, "rows": py * 2 + px // 2}

    sibling = {"aux": zx * 2 + 1 - c, "rows": rows}
    partner = {"aux": aux, "rows": y * 2 + 1 - xh}
    y_right, y_left = chip(x, (y + 1) % 4, z, c), chip(x, (y + 3) % 4, z, c)
    same = [{"aux": ((zx + e) % 8) * 2 + c, "rows": rows} for e in range(1, 8)]
    owners = [{"aux": aux, "rows": (rows + d) % 8} for d in range(1, 8)]
    across = {"aux": z * 4 + (1 - xl) * 2 + c, "rows": y * 2 + 1 - xh}

    loads = []
    for m in range(RB):
        load = pltpu.make_async_copy(t_hbm.at[:, m], t_v.at[m], t_sem.at[m])
        load.start()
        loads.append(load)

    barrier = pltpu.get_barrier_semaphore()
    greeted = same + [sibling] + owners + [across]
    for device in greeted:
        pl.semaphore_signal(barrier, inc=1, device_id=device, device_id_type=pl.DeviceIdType.MESH)

    for m in range(RB):
        picks[m, zx, c] = coeff_ref[sig_ref[m, aux]]
    lane = lax.broadcasted_iota(jnp.int32, (8, 128), 1)
    mine = jnp.zeros((8, 128), jnp.int32)
    for m in range(RB):
        for s in range(KS):
            mine = jnp.where(lane == m * KS + s, cols_ref[m, s], mine)
    cols_mine[...] = mine
    pl.semaphore_wait(barrier, len(greeted))

    sends = []

    def send(*args):
        copy = remote(*args)
        copy.start()
        sends.append(copy)

    for m in range(RB):
        block = picks.at[m, zx, c]
        for e in range(7):
            send(block, block, p_send.at[m, e], p_recv.at[m, e], same[e])
    send(cols_mine, cols_got, k_sem.at[0], k_sem.at[1], partner)

    def row_block(py, which, m):
        owner = xh if which == 0 else 1 - xh
        return h_all.at[(py * 2 + owner) * RB + m]

    def pass_on(m, which):
        block = row_block(y, which, m)
        send(block, block, y_send.at[m, which], y_recv.at[m, which], y_right)
        send(block, block, y_send.at[m, 2 + which], y_recv.at[m, 2 + which], y_left)

    def relay(m, which):
        if which == 0:
            block = row_block((y + 3) % 4, 0, m)
            remote(block, block, y_send.at[m, 0], y_recv.at[m, 0], y_left).wait_recv()
            send(block, block, y_send.at[m, 4], y_recv.at[m, 4], y_right)
        else:
            block = row_block((y + 1) % 4, 1, m)
            remote(block, block, y_send.at[m, 3], y_recv.at[m, 3], y_right).wait_recv()
            send(block, block, y_send.at[m, 5], y_recv.at[m, 5], y_left)

    def from_partner(m):
        block = row_block(y, 1, m)
        remote(block, block, x_send.at[m], x_recv.at[m], partner).wait_recv()
        pass_on(m, 1)

    for m in range(RB):
        for e in range(7):
            block = picks.at[m, (zx + 7 - e) % 8, c]
            remote(block, block, p_send.at[m, e], p_recv.at[m, e], same[e]).wait_recv()
        block = picks.at[m, :, c]
        send(block, block, b_send.at[m], b_recv.at[m], sibling)
        other = picks.at[m, :, 1 - c]
        remote(other, other, b_send.at[m], b_recv.at[m], sibling).wait_recv()
        loads[m].wait()

        def half(g, carry, m=m):
            chosen = (1 - g) * (1 - xh) + g * xh
            slab = jnp.concatenate(
                [t_v[m, pl.ds(chosen * 4, 4), q].reshape(4 * BS, BS) for q in range(16)], axis=1
            )
            weight = picks[m].reshape(16 * BS, OCC)
            value = jnp.dot(slab, weight, preferred_element_type=F32).astype(BF16)
            where = (1 - g) * (8 * RB + m) + g * (rows * RB + m)
            for p in range(4):
                h_all[where, :, p * OCC : (p + 1) * OCC] = value[p * BS : (p + 1) * BS]
            return carry

        lax.fori_loop(0, 2, half, 0)
        send(
            h_all.at[8 * RB + m],
            h_all.at[rows * RB + m],
            x_send.at[m],
            x_recv.at[m],
            partner,
        )
        pass_on(m, 0)
        if m >= 1:
            from_partner(m - 1)
        if m >= 2:
            relay(m - 2, 0)
    from_partner(RB - 1)
    for m in range(RB):
        if m >= RB - 2:
            relay(m, 0)
        relay(m, 1)

    remote(cols_mine, cols_got, k_sem.at[0], k_sem.at[1], partner).wait_recv()
    inward = pltpu.make_async_copy(cols_got, cols_sm, k_sem.at[2])
    inward.start()
    inward.wait()
    for m in range(RB):
        block = row_block((y + 3) % 4, 1, m)
        remote(block, block, y_send.at[m, 1], y_recv.at[m, 1], y_left).wait_recv()
        block = row_block((y + 1) % 4, 0, m)
        remote(block, block, y_send.at[m, 2], y_recv.at[m, 2], y_right).wait_recv()
        block = row_block((y + 2) % 4, 0, m)
        remote(block, block, y_send.at[m, 4], y_recv.at[m, 4], y_left).wait_recv()
        block = row_block((y + 2) % 4, 1, m)
        remote(block, block, y_send.at[m, 5], y_recv.at[m, 5], y_right).wait_recv()

    u = (1 - c) * x + c * z
    v = (1 - c) * z + c * x
    right1 = chip((x + 1 - c) % 4, y, (z + c) % 4, c)
    left1 = chip((x + 3 * (1 - c)) % 4, y, (z + 3 * c) % 4, c)
    right2 = chip((x + c) % 4, y, (z + 1 - c) % 4, c)
    left2 = chip((x + 3 * c) % 4, y, (z + 3 * (1 - c)) % 4, c)
    u_next, u_last, u_far = (u + 1) % 4, (u + 3) % 4, (u + 2) % 4
    v_next, v_last, v_far = (v + 1) % 4, (v + 3) % 4, (v + 2) % 4

    def products(m):
        def pair(i, carry):
            g, sp = i // (KS // 2), i % (KS // 2)
            left = h_all[(y * 2 + g) * RB + m]
            cols = [
                jnp.where(g == xh, cols_ref[m, sp * 2 + h], cols_sm[0, m * KS + sp * 2 + h])
                for h in range(2)
            ]
            right = jnp.concatenate([h_all[cols[0]], h_all[cols[1]]], axis=0)
            value = lax.dot_general(
                left, right, (((1,), (1,)), ((), ())), preferred_element_type=F32
            )
            for j in range(16):
                jz, jx, jc = j // 4, (j // 2) % 2, j % 2
                jx = g * 2 + jx
                ju, jv = (jx, jz) if jc == 0 else (jz, jx)
                for h in range(2):
                    part[m, jc, ju, jv, sp * 2 + h] = value[
                        j * 8 : j * 8 + 8, h * BS : (h + 1) * BS
                    ]
            return carry

        lax.fori_loop(0, KS, pair, 0)
        send(part.at[m, 1 - c], core_in.at[m], c_send.at[m], c_recv.at[m], sibling)

    def stage1(m):
        remote(core_in.at[m], core_in.at[m], c_send.at[m], c_recv.at[m], sibling).wait_recv()

        def add(i, carry):
            part[m, c, i] = part[m, c, i] + core_in[m, i]
            return carry

        lax.fori_loop(0, 4, add, 0)
        far = part.at[m, c, u_far]
        send(far.at[0:2], r1a.at[m, 0], r_send.at[m, 0], r_recv.at[m, 0], right1)
        send(far.at[2:4], r1a.at[m, 1], r_send.at[m, 1], r_recv.at[m, 1], left1)

    def arrive(buffer, m, i, device):
        remote(buffer, buffer, r_send.at[m, i], r_recv.at[m, i], device).wait_recv()

    def stage2(m):
        arrive(r1a.at[m, 0], m, 0, left1)
        part[m, c, u_next, 0:2] = part[m, c, u_next, 0:2] + r1a[m, 0]
        send(part.at[m, c, u_next], r1b.at[m, 0], r_send.at[m, 2], r_recv.at[m, 2], right1)
        arrive(r1a.at[m, 1], m, 1, right1)
        part[m, c, u_last, 2:4] = part[m, c, u_last, 2:4] + r1a[m, 1]
        send(part.at[m, c, u_last], r1b.at[m, 1], r_send.at[m, 3], r_recv.at[m, 3], left1)

    def stage3(m):
        arrive(r1b.at[m, 0], m, 2, left1)
        arrive(r1b.at[m, 1], m, 3, right1)
        part[m, c, u] = part[m, c, u] + r1b[m, 0] + r1b[m, 1]
        far = part.at[m, c, u, v_far]
        send(far.at[0:6], r2a.at[m, 0], r_send.at[m, 4], r_recv.at[m, 4], right2)
        send(far.at[6:12], r2a.at[m, 1], r_send.at[m, 5], r_recv.at[m, 5], left2)

    def stage4(m):
        arrive(r2a.at[m, 0], m, 4, left2)
        part[m, c, u, v_next, 0:6] = part[m, c, u, v_next, 0:6] + r2a[m, 0]
        send(part.at[m, c, u, v_next], r2b.at[m, 0], r_send.at[m, 6], r_recv.at[m, 6], right2)
        arrive(r2a.at[m, 1], m, 5, right2)
        part[m, c, u, v_last, 6:12] = part[m, c, u, v_last, 6:12] + r2a[m, 1]
        send(part.at[m, c, u, v_last], r2b.at[m, 1], r_send.at[m, 7], r_recv.at[m, 7], left2)

    def stage5(m):
        arrive(r2b.at[m, 0], m, 6, left2)
        arrive(r2b.at[m, 1], m, 7, right2)
        red[1 + m * KS : 1 + (m + 1) * KS] = part[m, c, u, v] + r2b[m, 0] + r2b[m, 1]

    red[0] = jnp.zeros((8, BS), F32)
    stages = [products, stage1, stage2, stage3, stage4, stage5]
    for t in range(RB + 5):
        for lag, stage in enumerate(stages):
            if 0 <= t - lag < RB:
                stage(t - lag)

    for d in range(7):
        owner = (rows + d + 1) % 8
        for s in range(CAP):
            abuf[d, s] = red[slot_ref[owner, s]]
        send(
            abuf.at[d],
            out_ref.at[pl.ds(rows * CAP, CAP)],
            a_send.at[d],
            a_recv.at[d],
            owners[d],
        )
    for s in range(CAP):
        out_ref[rows * CAP + s] = red[slot_ref[rows, s]]
    for d in range(7):
        landed = out_ref.at[pl.ds(((rows + 7 - d) % 8) * CAP, CAP)]
        remote(abuf.at[d], landed, a_send.at[d], a_recv.at[d], owners[d]).wait_recv()
    for copy in sends:
        copy.wait_send()


def slots_of(owner_ids, total):
    count = owner_ids.shape[0]
    at = jnp.arange(count, dtype=jnp.int32)
    same = (owner_ids[:, None] == owner_ids[None, :]) & (at[None, :] < at[:, None])
    target = owner_ids * CAP + jnp.sum(same.astype(jnp.int32), axis=1)
    place = jnp.arange(total * CAP, dtype=jnp.int32)
    hit = target[None, :] == place[:, None]
    return jnp.sum(jnp.where(hit, at[None, :] + 1, 0), axis=1).reshape(total, CAP)


def per_device(three_center, coeffs, sig_blocks, k_columns, owners):
    slots = slots_of(owners[:, 0], 8)
    vmem, smem = pltpu.VMEM, pltpu.SMEM
    dma = pltpu.SemaphoreType.DMA
    return pl.pallas_call(
        kernel,
        out_shape=jax.ShapeDtypeStruct((8 * CAP, 8, BS), F32),
        in_specs=[
            pl.BlockSpec(memory_space=pl.ANY),
            pl.BlockSpec(memory_space=vmem),
            pl.BlockSpec(memory_space=smem),
            pl.BlockSpec(memory_space=smem),
            pl.BlockSpec(memory_space=smem),
        ],
        out_specs=pl.BlockSpec(memory_space=vmem),
        scratch_shapes=[
            vmem((RB, 8, 16, BS, BS), BF16),
            vmem((RB, 8, 2, BS, OCC), BF16),
            vmem((9 * RB, BS, 4 * OCC), BF16),
            vmem((8, 128), jnp.int32),
            vmem((8, 128), jnp.int32),
            smem((8, 128), jnp.int32),
            vmem((RB, 2, 4, 4, KS, 8, BS), F32),
            vmem((RB, 4, 4, KS, 8, BS), F32),
            vmem((RB, 2, 2, KS, 8, BS), F32),
            vmem((RB, 2, 4, KS, 8, BS), F32),
            vmem((RB, 2, KS // 2, 8, BS), F32),
            vmem((RB, 2, KS, 8, BS), F32),
            vmem((1 + RB * KS, 8, BS), F32),
            vmem((7, CAP, 8, BS), F32),
            dma((RB,)),
            dma((RB, 7)),
            dma((RB, 7)),
            dma((RB,)),
            dma((RB,)),
            dma((RB,)),
            dma((RB,)),
            dma((3,)),
            dma((RB, 6)),
            dma((RB, 6)),
            dma((RB,)),
            dma((RB,)),
            dma((RB, 8)),
            dma((RB, 8)),
            dma((7,)),
            dma((7,)),
        ],
        compiler_params=pltpu.CompilerParams(
            collective_id=0, has_side_effects=True, vmem_limit_bytes=60 * 1024 * 1024
        ),
    )(
        three_center,
        coeffs.reshape(BLK_DEV, BS, OCC),
        sig_blocks,
        k_columns,
        slots,
    )


def solution(mesh):
    return jax.shard_map(
        per_device,
        mesh=mesh,
        in_specs=(
            P("aux", "rows", None, None, None),
            P("aux", None),
            P("rows", None),
            P("rows", None),
            P("rows", None),
        ),
        out_specs=P("rows", "aux", None),
        check_vma=False,
    )
```
